32 devices in a mesh: pair: 2 (over y), blk: 16 (over z, x, core).
Axes of the slice: x: 2, y: 2, z: 4, core: 2. Of those that a mesh axis runs over, the one named last changes fastest.
Arguments:
- amps: bfloat16 [2048, 80200], P(('blk', 'pair')), may hold values from -6 to 6
- ints: bfloat16 [256, 80200], P('blk', 'pair'), may hold values from -0.015625 to 0.015625
- block_of: int32 [16], replicated, may hold values from 0 to 15, each once
- pair_rows: int32 [2048, 2], P(('blk', 'pair')), may hold values from 0 to 119
- occ_energy: float32 [120], replicated, may hold values from -2 to -0.5
- vir_pair_energy: float32 [256], replicated, may hold values from 1 to 6
Outputs:
- new_amps: float32 [2048, 256], P(('blk', 'pair'))
The draws below stay inside these ranges and needn't reach their ends.
Inputs may be any that keep to these rules, and one draw needn't show every extreme that they name: `block_of`: each of 0 to 15 once.
All inputs are finite; a program needn't handle non-finite values.
Results may differ from the reference program's by a relative error of at most 0.0003.
Values may be sent and summed in bfloat16 or wider, within the bound.
No kernel may reach another device: no remote copies, remote signals or barrier semaphores. Data moves between devices by JAX's collectives and lax.ppermute only.
A program may use at most 128 MiB of HBM per device.

```python
import jax
import jax.numpy as jnp
from jax import lax

NO = 120
NV = 400
CD = 80200
AB_DEV = 16
BLOCKS = 16
OP = 2048
AB = 256


def with_ends(array, key, least, top_value):
    shape = array.shape
    place = [jax.random.randint(jax.random.fold_in(key, axis), (), 0, shape[axis]) for axis in range(len(shape))]
    array = array.at[tuple(place)].set(least)
    longest = shape.index(max(shape))
    place[longest] = (place[longest] + 1) % shape[longest]
    return array.at[tuple(place)].set(top_value)


def level_of(rng, shape, shards, smallest, top_value):
    gain, own = 1.0, jax.random.fold_in(rng, 6)
    for axis_at, parts in shards:
        heights = jnp.exp(jax.random.uniform(jax.random.fold_in(own, axis_at), (parts,), jnp.float32, smallest / len(shards), top_value / len(shards)))
        gain = gain * jnp.repeat(heights, shape[axis_at] // parts).reshape([-1 if axis == axis_at else 1 for axis in range(len(shape))])
    return gain


def noise(key, dims, spread, most, pieces=(), kind=jnp.bfloat16):
    entries = jax.random.normal(key, dims, jnp.float32) * spread
    if len(pieces) > 0:
        entries = level_of(key, dims, pieces, -0.22, 0.18) * entries
    return jnp.clip(entries, min=-most, max=most).astype(kind)


def setup_inputs(seed: int = 0) -> dict:
    key_of = jax.random.split(jax.random.key(seed), 7)
    return {
        "amps": noise(key_of[0], (OP, CD), 1.0, 6.0, ((0, 32),)),
        "ints": noise(key_of[1], (AB, CD), (2 * CD) ** -0.5, 0.015625, ((0, 16), (1, 2))),
        "block_of": jax.random.permutation(key_of[2], BLOCKS).astype(jnp.int32),
        "pair_rows": with_ends(jax.random.randint(key_of[3], (OP, 2), 0, NO), jax.random.fold_in(key_of[3], 1), 0, NO - 1).astype(jnp.int32),
        "occ_energy": jnp.clip(jax.random.uniform(key_of[4], (NO,), jnp.float32, -2.0, -0.5), -2.0, -0.5),
        "vir_pair_energy": jnp.clip(jax.random.uniform(key_of[5], (AB,), jnp.float32, 1.0, 6.0), 1.0, 6.0),
    }


def reference(amps, ints, block_of, pair_rows, occ_energy, vir_pair_energy):
    column = jnp.arange(ints.shape[1], dtype=jnp.int32)[None, :]
    weight = jnp.where(column < NV, 1.0, 2.0).astype(jnp.bfloat16)
    weighted_ints = ints * weight
    ladder_raw = lax.dot_general(amps, weighted_ints, (((1,), (1,)), ((), ())), preferred_element_type=jnp.float32)
    grouped = ladder_raw.reshape(OP, BLOCKS, AB_DEV)
    ladder = jnp.zeros_like(grouped).at[:, block_of].set(grouped).reshape(OP, AB)
    occupied = occ_energy[pair_rows[:, 0]] + occ_energy[pair_rows[:, 1]]
    denominator = vir_pair_energy[None, :] - occupied[:, None]
    return ladder / denominator
```

```python
import functools

import jax
import jax.numpy as jnp
from jax import lax
from jax.experimental import pallas as pl
from jax.experimental.pallas import tpu as pltpu
from jax.sharding import PartitionSpec as P

NV = 400
LANE = 128
CORES = 2
AXES = ("pair", "blk")


def ring_of(chips):
    nx = 1
    while nx * nx * 4 <= chips:
        nx *= 2
    nz = chips // nx
    if nx < 2 or nz % 2:
        return list(range(chips))
    order = [z * nx for z in range(nz)]
    for k, z in enumerate(range(nz - 1, -1, -1)):
        xs = range(1, nx) if k % 2 == 0 else range(nx - 1, 0, -1)
        order += [z * nx + x for x in xs]
    return order


def chunks_of(units):
    if units < 60:
        return [units - units // 3, units // 3] if units > 3 else [units]
    first = [units * f // 100 // 10 * 10 for f in (32, 32, 20)]
    return first + [units - sum(first)]


def tile_of(units):
    return max(d for d in range(1, 17) if units % d == 0) if units > 24 else units


def matmul_kernel(n_amps, n_ints, rows, sub, has_acc, pos_ref, *refs):
    amps, refs = refs[:n_amps], refs[n_amps:]
    ints, refs = refs[:n_ints], refs[n_ints:]
    acc_in = ()
    if has_acc:
        acc_in, refs = refs[:n_amps], refs[n_amps:]
    outs, (table, total) = refs[:n_amps], refs[n_amps:]
    step = pl.program_id(0)
    for j, ref in enumerate(ints):
        for h in range(CORES):
            at = pl.multiple_of(pos_ref[CORES * j + h] * sub, sub)
            table[pl.ds(at, sub), :] = ref[h * sub : (h + 1) * sub, :]
    left = jnp.concatenate([ref[...] for ref in amps], axis=0)
    product = lax.dot_general(
        left, table[...], (((1,), (1,)), ((), ())), preferred_element_type=jnp.float32
    )

    @pl.when(step == 0)
    def _():
        if has_acc:
            for g in range(n_amps):
                part = slice(g * rows, (g + 1) * rows)
                total[part, :] = acc_in[g][...] + product[part, :]
        else:
            total[...] = product

    @pl.when(step > 0)
    def _():
        total[...] += product

    @pl.when(step == pl.num_programs(0) - 1)
    def _():
        for g in range(n_amps):
            outs[g][...] = total[g * rows : (g + 1) * rows, :]


def chunk_matmul(pos, amps, ints, acc):
    rows, width = amps[0].shape
    sub = ints[0].shape[0] // CORES
    cols = len(ints) * CORES * sub
    units = width // LANE
    tile = tile_of(units) * LANE
    n = len(amps)
    whole = pl.BlockSpec((rows, cols), lambda k, s: (0, 0))
    spec = pltpu.PrefetchScalarGridSpec(
        num_scalar_prefetch=1,
        grid=(width // tile,),
        in_specs=[pl.BlockSpec((rows, tile), lambda k, s: (0, k))] * n
        + [pl.BlockSpec((CORES * sub, tile), lambda k, s: (0, k))] * len(ints)
        + [whole] * len(acc),
        out_specs=[whole] * n,
        scratch_shapes=[
            pltpu.VMEM((cols, tile), jnp.bfloat16),
            pltpu.VMEM((n * rows, cols), jnp.float32),
        ],
    )
    return pl.pallas_call(
        functools.partial(matmul_kernel, n, len(ints), rows, sub, len(acc) > 0),
        grid_spec=spec,
        out_shape=[jax.ShapeDtypeStruct((rows, cols), jnp.float32)] * n,
        compiler_params=pltpu.CompilerParams(dimension_semantics=("arbitrary",)),
        cost_estimate=pl.CostEstimate(
            flops=2 * n * rows * cols * width,
            bytes_accessed=2 * (n * rows + cols) * width,
            transcendentals=0,
        ),
        name="ladder_chunk",
    )(pos, *amps, *ints, *acc)


def solution(mesh):
    n_pair, n_blk = mesh.shape["pair"], mesh.shape["blk"]
    chips = n_blk // CORES
    ring = ring_of(chips)

    def device(pair, chip, core):
        return pair * n_blk + chip * CORES + core

    def everywhere(target):
        return [
            (device(p, ch, c), device(*target(p, ch, c)))
            for p in range(n_pair)
            for ch in range(chips)
            for c in range(CORES)
        ]

    place = {ch: i for i, ch in enumerate(ring)}
    forward = everywhere(lambda p, ch, c: (p, ring[(place[ch] + 1) % chips], c))
    backward = everywhere(lambda p, ch, c: (p, ring[(place[ch] - 1) % chips], c))
    mates = [(d, e) for d in range(n_pair) for e in range(CORES)]
    to_mate = {
        (d, e): everywhere(lambda p, ch, c: ((p + d) % n_pair, ch, c ^ e)) for d, e in mates
    }

    def per_device(amps, ints, block_of, pair_rows, occ_energy, vir_pair_energy):
        rows, total_width = amps.shape
        sub, width = ints.shape
        starts = [p * width // LANE * LANE for p in range(n_pair)]
        reach = max((p + 1) * width - starts[p] for p in range(n_pair))
        units = -(-reach // (LANE * CORES))
        half = units * LANE
        sizes = [u * LANE for u in chunks_of(units)]
        offsets = [sum(sizes[:j]) for j in range(len(sizes))]
        count = len(sizes)
        pair, blk = lax.axis_index("pair"), lax.axis_index("blk")
        chip, core = blk // CORES, blk % CORES
        which = pair * CORES + core

        def amps_branch(p, c, j, x):
            out = []
            for d, e in mates:
                at = starts[(p + d) % n_pair] + (c ^ e) * half + offsets[j]
                end = min(at + sizes[j], total_width)
                piece = lax.slice(x, (0, at), (rows, end))
                out.append(jnp.pad(piece, ((0, 0), (0, at + sizes[j] - end))))
            return out

        def ints_branch(p, c, x):
            column = p * width + lax.broadcasted_iota(jnp.int32, (1, width), 1)
            weight = jnp.where(column < NV, 1.0, 2.0).astype(jnp.bfloat16)
            shift = p * width - starts[p]
            x = jnp.pad(x * weight, ((0, 0), (shift, CORES * half - width - shift)))
            out = []
            for j in range(count):
                for core_of in (c, c ^ 1):
                    at = core_of * half + offsets[j]
                    out.append(lax.slice(x, (0, at), (sub, at + sizes[j])))
            return out

        grid = [(p, c) for p in range(n_pair) for c in range(CORES)]

        def pack_amps(j):
            return lax.switch(which, [functools.partial(amps_branch, p, c, j) for p, c in grid], amps)

        packed = [pack_amps(0)]
        split = lax.switch(which, [functools.partial(ints_branch, p, c) for p, c in grid], ints)

        def exchange(parts):
            return [
                part if m == (0, 0) else lax.ppermute(part, AXES, to_mate[m])
                for m, part in zip(mates, parts)
            ]

        left = [exchange(packed[0])]
        mine = []
        for j in range(count):
            other = lax.ppermute(split[2 * j + 1], AXES, to_mate[(0, 1)])
            mine.append(jnp.concatenate([split[2 * j], other], axis=0))
        left += [exchange(pack_amps(j)) for j in range(1, count)]

        long, short = chips // 2, chips - 1 - chips // 2
        right = []
        for j in range(count):
            ahead, behind = (long, short) if j % 2 == 0 else (short, long)
            fwd, bwd = [mine[j]], [mine[j]]
            for s in range(max(ahead, behind)):
                if s < ahead:
                    fwd.append(lax.ppermute(fwd[-1], AXES, forward))
                if s < behind:
                    bwd.append(lax.ppermute(bwd[-1], AXES, backward))
            right.append(fwd + bwd[:0:-1])

        order = jnp.array(ring, jnp.int32)
        here = jnp.argmax(order == chip)
        behind_me = order[(here - jnp.arange(chips)) % chips]
        stored = jnp.stack([behind_me * CORES + core, behind_me * CORES + 1 - core], axis=1)
        pos = block_of[stored.reshape(-1)]

        acc = []
        for j in range(count):
            acc = chunk_matmul(pos, left[j], right[j], acc)

        ladder = acc[0]
        for m, part in list(zip(mates, acc))[1:]:
            d, e = m
            back = everywhere(lambda p, ch, c: ((p - d) % n_pair, ch, c ^ e))
            ladder = ladder + lax.ppermute(part, AXES, back)
        levels = lax.broadcasted_iota(jnp.int32, (1, 1, occ_energy.shape[0]), 2)
        one_hot = (pair_rows[:, :, None] == levels).astype(jnp.float32)
        occupied = jnp.sum(one_hot * occ_energy[None, None, :], axis=(1, 2))
        denominator = vir_pair_energy[None, :] - occupied[:, None]
        return ladder / denominator

    placed = (P(("blk", "pair"), None), P("blk", "pair"), P(), P(("blk", "pair"), None), P(), P())
    return jax.shard_map(
        per_device, mesh=mesh, in_specs=placed, out_specs=P(("blk", "pair"), None), check_vma=False
    )
```

```python
import functools

import jax
import jax.numpy as jnp
from jax import lax
from jax.experimental import pallas as pl
from jax.experimental.pallas import tpu as pltpu
from jax.sharding import PartitionSpec as P


NV = 400
LANE = 128
CORES = 2
AXES = ("pair", "blk")


def ring_of(chips):
    nx = 1
    while nx * nx * 4 <= chips:
        nx *= 2
    nz = chips // nx
    if nx < 2 or nz % 2:
        return list(range(chips))
    order = [z * nx for z in range(nz)]
    for k, z in enumerate(range(nz - 1, -1, -1)):
        xs = range(1, nx) if k % 2 == 0 else range(nx - 1, 0, -1)
        order += [z * nx + x for x in xs]
    return order


def chunks_of(units, n_pair):
    if units < 60:
        return [units - units // 3, units // 3], 0
    wide = units * 9 // 100 if n_pair == 2 else 0
    first = [units * f // 100 // 10 * 10 for f in (27, 27, 27)]
    return first + [units - wide - sum(first)], wide


def tile_of(units):
    return max(d for d in range(1, 17) if units % d == 0) if units > 24 else units


def matmul_kernel(n_amps, n_ints, rows, sub, has_acc, pos_ref, *refs):
    amps, refs = refs[:n_amps], refs[n_amps:]
    ints, refs = refs[:n_ints], refs[n_ints:]
    acc_in = ()
    if has_acc:
        acc_in, refs = refs[:n_amps], refs[n_amps:]
    outs, (table, total) = refs[:n_amps], refs[n_amps:]
    step = pl.program_id(0)
    for j, ref in enumerate(ints):
        for h in range(CORES):
            at = pl.multiple_of(pos_ref[CORES * j + h] * sub, sub)
            table[pl.ds(at, sub), :] = ref[h * sub : (h + 1) * sub, :]
    left = jnp.concatenate([ref[...] for ref in amps], axis=0)
    product = lax.dot_general(
        left, table[...], (((1,), (1,)), ((), ())), preferred_element_type=jnp.float32
    )

    @pl.when(step == 0)
    def _():
        if has_acc:
            for g in range(n_amps):
                part = slice(g * rows, (g + 1) * rows)
                total[part, :] = acc_in[g][...] + product[part, :]
        else:
            total[...] = product

    @pl.when(step > 0)
    def _():
        total[...] += product

    @pl.when(step == pl.num_programs(0) - 1)
    def _():
        for g in range(n_amps):
            outs[g][...] = total[g * rows : (g + 1) * rows, :]


def chunk_matmul(pos, amps, ints, acc):
    rows, width = amps[0].shape
    sub = ints[0].shape[0] // CORES
    cols = len(ints) * CORES * sub
    units = width // LANE
    tile = tile_of(units) * LANE
    n = len(amps)
    whole = pl.BlockSpec((rows, cols), lambda k, s: (0, 0))
    spec = pltpu.PrefetchScalarGridSpec(
        num_scalar_prefetch=1,
        grid=(width // tile,),
        in_specs=[pl.BlockSpec((rows, tile), lambda k, s: (0, k))] * n
        + [pl.BlockSpec((CORES * sub, tile), lambda k, s: (0, k))] * len(ints)
        + [whole] * len(acc),
        out_specs=[whole] * n,
        scratch_shapes=[
            pltpu.VMEM((cols, tile), jnp.bfloat16),
            pltpu.VMEM((n * rows, cols), jnp.float32),
        ],
    )
    return pl.pallas_call(
        functools.partial(matmul_kernel, n, len(ints), rows, sub, len(acc) > 0),
        grid_spec=spec,
        out_shape=[jax.ShapeDtypeStruct((rows, cols), jnp.float32)] * n,
        compiler_params=pltpu.CompilerParams(dimension_semantics=("arbitrary",)),
        cost_estimate=pl.CostEstimate(
            flops=2 * n * rows * cols * width,
            bytes_accessed=2 * (n * rows + cols) * width,
            transcendentals=0,
        ),
        name="ladder_chunk",
    )(pos, *amps, *ints, *acc)


def solution(mesh):
    n_pair, n_blk = mesh.shape["pair"], mesh.shape["blk"]
    chips = n_blk // CORES
    ring = ring_of(chips)
    long, short = chips // 2, chips - 1 - chips // 2

    def device(pair, chip, core):
        return pair * n_blk + chip * CORES + core

    def everywhere(target):
        return [
            (device(p, ch, c), device(*target(p, ch, c)))
            for p in range(n_pair)
            for ch in range(chips)
            for c in range(CORES)
        ]

    place = {ch: i for i, ch in enumerate(ring)}
    forward = everywhere(lambda p, ch, c: (p, ring[(place[ch] + 1) % chips], c))
    backward = everywhere(lambda p, ch, c: (p, ring[(place[ch] - 1) % chips], c))
    mates = [(d, e) for d in range(n_pair) for e in range(CORES)]
    to_mate = {
        (d, e): everywhere(lambda p, ch, c: ((p + d) % n_pair, ch, c ^ e)) for d, e in mates
    }
    grid = [(p, c) for p in range(n_pair) for c in range(CORES)]

    def send(x, pairs):
        return lax.ppermute(x, AXES, pairs)

    def choose(which, branch, *operands):
        return lax.switch(which, [functools.partial(branch, p, c) for p, c in grid], *operands)

    def per_device(amps, ints, block_of, pair_rows, occ_energy, vir_pair_energy):
        rows, total_width = amps.shape
        sub, width = ints.shape
        starts = [p * width // LANE * LANE for p in range(n_pair)]
        reach = max((p + 1) * width - starts[p] for p in range(n_pair))
        units = -(-reach // (LANE * CORES))
        half = units * LANE
        narrow, wide = chunks_of(units, n_pair)
        sizes = [u * LANE for u in narrow + ([wide] if wide else [])]
        offsets = [sum(sizes[:j]) for j in range(len(sizes))]
        count = len(narrow)
        pair, blk = lax.axis_index("pair"), lax.axis_index("blk")
        chip, core = blk // CORES, blk % CORES
        which = pair * CORES + core

        def amps_at(x, p, c, j):
            at = starts[p] + c * half + offsets[j]
            end = min(at + sizes[j], total_width)
            return jnp.pad(lax.slice(x, (0, at), (rows, end)), ((0, 0), (0, at + sizes[j] - end)))

        def amps_branch(j, some, p, c, x):
            return [amps_at(x, (p + d) % n_pair, c ^ e, j) for d, e in some]

        def wide_branch(p, c, x):
            return [
                jnp.concatenate(
                    [amps_at(x, (p + d) % n_pair, c ^ e, count) for d in range(n_pair)], axis=1
                )
                for e in range(CORES)
            ]

        def ints_branch(j, p, c, *slabs):
            shift = p * width - starts[p]
            first = c * half + offsets[j] - shift
            low, high = max(first, 0), min(first + sizes[j], width)
            column = p * width + low + lax.broadcasted_iota(jnp.int32, (1, high - low), 1)
            weight = jnp.where(column < NV, 1.0, 2.0).astype(jnp.bfloat16)
            both = jnp.concatenate([lax.slice(x, (0, low), (sub, high)) for x in slabs], axis=0)
            return jnp.pad(both * weight, ((0, 0), (low - first, first + sizes[j] - high)))

        def round_trip(piece, even):
            ahead, behind = (long, short) if even else (short, long)
            fwd, bwd = [piece], [piece]
            for s in range(1, max(ahead, behind) + 1):
                if s <= ahead:
                    fwd.append(send(fwd[-1], forward))
                if s <= behind:
                    bwd.append(send(bwd[-1], backward))
            return fwd + bwd[:0:-1]

        twin = send(ints, to_mate[(0, 1)])
        near = [m for m in mates if m[0] == 0]
        far = [m for m in mates if m[0] != 0]
        left, right = [], []
        for j in range(count):
            parts = choose(which, functools.partial(amps_branch, j, far), amps)
            away = [send(x, to_mate[m]) for m, x in zip(far, parts)]
            parts = choose(which, functools.partial(amps_branch, j, near), amps)
            left.append([parts[0], send(parts[1], to_mate[(0, 1)])] + away)
            piece = choose(which, functools.partial(ints_branch, j), ints, twin)
            right.append(round_trip(piece, j % 2 == 0))
        if wide:
            piece = choose(which, functools.partial(ints_branch, count), ints, twin)
            others = [send(piece, to_mate[(n_pair - d, 0)]) for d in range(1, n_pair)]
            piece = jnp.concatenate([piece] + others, axis=1)
            right.append(round_trip(piece, False))
            parts = choose(which, wide_branch, amps)
            left.append([parts[0], send(parts[1], to_mate[(0, 1)])])

        order = jnp.array(ring, jnp.int32)
        here = jnp.argmax(order == chip)
        behind_me = order[(here - jnp.arange(chips)) % chips]
        stored = jnp.stack([behind_me * CORES + core, behind_me * CORES + 1 - core], axis=1)
        pos = block_of[stored.reshape(-1)]

        acc = []
        for j in range(count):
            acc = chunk_matmul(pos, left[j], right[j], acc)
        ladder = acc[0]
        for (d, e), part in list(zip(mates, acc))[1:]:
            ladder = ladder + send(part, to_mate[((n_pair - d) % n_pair, e)])
        if wide:
            acc = chunk_matmul(pos, left[count], right[count], [])
            ladder = ladder + acc[0] + send(acc[1], to_mate[(0, 1)])
        levels = lax.broadcasted_iota(jnp.int32, (1, 1, occ_energy.shape[0]), 2)
        one_hot = (pair_rows[:, :, None] == levels).astype(jnp.float32)
        occupied = jnp.sum(one_hot * occ_energy[None, None, :], axis=(1, 2))
        denominator = vir_pair_energy[None, :] - occupied[:, None]
        return ladder / denominator

    placed = (P(("blk", "pair"), None), P("blk", "pair"), P(), P(("blk", "pair"), None), P(), P())
    return jax.shard_map(
        per_device, mesh=mesh, in_specs=placed, out_specs=P(("blk", "pair"), None), check_vma=False
    )
```

```python
import functools

import jax
import jax.numpy as jnp
from jax import lax
from jax.experimental import pallas as pl
from jax.experimental.pallas import tpu as pltpu
from jax.sharding import PartitionSpec as P


NV = 400
LANE = 128
CORES = 2
LARGE = 40
AXES = ("pair", "blk")


def ring_of(chips):
    nx = 1
    while nx * nx * 4 <= chips:
        nx *= 2
    nz = chips // nx
    if nx < 2 or nz % 2:
        return list(range(chips))
    order = [z * nx for z in range(nz)]
    for k, z in enumerate(range(nz - 1, -1, -1)):
        xs = range(1, nx) if k % 2 == 0 else range(nx - 1, 0, -1)
        order += [z * nx + x for x in xs]
    return order


def chunks_of(units, n_pair):
    if units < 60:
        return [units - units // 3, units // 3], 0
    wide = units * 7 // 100 if n_pair == 2 else 0
    rest = units - wide
    first = [rest * share // 1000 for share in (347, 347, 191)]
    return first + [rest - sum(first)], wide


def leads_forward(chunk):
    return chunk in (0, 2)


def tile_of(units):
    return max(d for d in range(1, 29) if units % d == 0) if units > 28 else units


def tiled_kernel(n_amps, n_ints, rows, sub, has_acc, pos_ref, *refs):
    amps, refs = refs[:n_amps], refs[n_amps:]
    ints, refs = refs[:n_ints], refs[n_ints:]
    acc_in = ()
    if has_acc:
        acc_in, refs = refs[:n_amps], refs[n_amps:]
    outs, (table, total) = refs[:n_amps], refs[n_amps:]
    step = pl.program_id(0)
    for j, ref in enumerate(ints):
        for h in range(CORES):
            at = pl.multiple_of(pos_ref[CORES * j + h] * sub, sub)
            table[pl.ds(at, sub), :] = ref[h * sub : (h + 1) * sub, :]
    left = jnp.concatenate([ref[...] for ref in amps], axis=0)
    product = lax.dot_general(
        left, table[...], (((1,), (1,)), ((), ())), preferred_element_type=jnp.float32
    )

    @pl.when(step == 0)
    def _():
        if has_acc:
            for g in range(n_amps):
                part = slice(g * rows, (g + 1) * rows)
                total[part, :] = acc_in[g][...] + product[part, :]
        else:
            total[...] = product

    @pl.when(step > 0)
    def _():
        total[...] += product

    @pl.when(step == pl.num_programs(0) - 1)
    def _():
        for g in range(n_amps):
            outs[g][...] = total[g * rows : (g + 1) * rows, :]


def tiled_matmul(pos, amps, ints, acc):
    rows, width = amps[0].shape
    sub = ints[0].shape[0] // CORES
    cols = len(ints) * CORES * sub
    units = width // LANE
    tile = tile_of(units) * LANE
    n = len(amps)
    whole = pl.BlockSpec((rows, cols), lambda k, s: (0, 0))
    spec = pltpu.PrefetchScalarGridSpec(
        num_scalar_prefetch=1,
        grid=(width // tile,),
        in_specs=[pl.BlockSpec((rows, tile), lambda k, s: (0, k))] * n
        + [pl.BlockSpec((CORES * sub, tile), lambda k, s: (0, k))] * len(ints)
        + [whole] * len(acc),
        out_specs=[whole] * n,
        scratch_shapes=[
            pltpu.VMEM((cols, tile), jnp.bfloat16),
            pltpu.VMEM((n * rows, cols), jnp.float32),
        ],
    )
    return pl.pallas_call(
        functools.partial(tiled_kernel, n, len(ints), rows, sub, len(acc) > 0),
        grid_spec=spec,
        out_shape=[jax.ShapeDtypeStruct((rows, cols), jnp.float32)] * n,
        compiler_params=pltpu.CompilerParams(dimension_semantics=("arbitrary",), vmem_limit_bytes=24 << 20),
        cost_estimate=pl.CostEstimate(
            flops=2 * n * rows * cols * width,
            bytes_accessed=2 * (n * rows + cols) * width,
            transcendentals=0,
        ),
        name="ladder_chunk",
    )(pos, *amps, *ints, *acc)


def matmul_kernel(layout, rows, sub, spans, n_acc, at_ref, *refs):
    n_amps, n_ints = layout
    amps, refs = refs[:n_amps], refs[n_amps:]
    ints, refs = refs[:n_ints], refs[n_ints:]
    acc_in, refs = refs[:n_acc], refs[n_acc:]
    outs, (left, right, total, tile_sem, acc_sem) = refs[:n_amps], refs[n_amps:]
    acc_copies = [
        pltpu.make_async_copy(ref, total.at[pl.ds(g * rows, rows), :], acc_sem.at[g])
        for g, ref in enumerate(acc_in)
    ]
    copies = []
    for t, (start, size) in enumerate(spans):
        here = pl.ds(start, size)
        sources = []
        for g, ref in enumerate(amps):
            if ref.shape[1] == left.shape[1]:
                source = ref.at[:, here]
            else:
                source = ref.at[:, pl.ds(pl.multiple_of(at_ref[0] + start, LANE), size)]
            sources.append((source, left.at[pl.ds(g * rows, rows), here]))
        for j, ref in enumerate(ints):
            for h in range(CORES):
                row = pl.multiple_of(at_ref[1 + CORES * j + h] * sub, sub)
                sources.append((ref.at[pl.ds(h * sub, sub), here], right.at[pl.ds(row, sub), here]))
        copies.append(
            [pltpu.make_async_copy(a, b, tile_sem.at[t, i]) for i, (a, b) in enumerate(sources)]
        )
    for group in copies:
        for copy in group:
            copy.start()
    for copy in acc_copies:
        copy.start()
    product = None
    for (start, size), group in zip(spans, copies):
        for copy in group:
            copy.wait()
        here = slice(start, start + size)
        part = lax.dot_general(
            left[:, here], right[:, here], (((1,), (1,)), ((), ())), preferred_element_type=jnp.float32
        )
        product = part if product is None else product + part
    for copy in acc_copies:
        copy.wait()
    for g in range(n_amps):
        part = slice(g * rows, (g + 1) * rows)
        outs[g][...] = total[part, :] + product[part, :] if n_acc else product[part, :]


def chunk_matmul(at, amps, ints, acc, width):
    if amps[0].shape[1] == width:
        return tiled_matmul(at[1:], amps, ints, acc)
    amps, ints = ([pltpu.with_memory_space_constraint(x, pltpu.HBM) for x in part] for part in (amps, ints))
    rows = amps[0].shape[0]
    sub = ints[0].shape[0] // CORES
    cols = len(ints) * CORES * sub
    n = len(amps)
    units = width // LANE
    pieces = max(1, units // 12)
    ends = [units * k // pieces * LANE for k in range(pieces + 1)]
    spans = [(a, b - a) for a, b in zip(ends, ends[1:])]
    whole = pl.BlockSpec((rows, cols), lambda *_: (0, 0))
    anywhere = pl.BlockSpec(memory_space=pl.ANY)
    spec = pltpu.PrefetchScalarGridSpec(
        num_scalar_prefetch=1,
        grid=(1,),
        in_specs=[anywhere] * (n + len(ints) + len(acc)),
        out_specs=[whole] * n,
        scratch_shapes=[
            pltpu.VMEM((n * rows, width), jnp.bfloat16),
            pltpu.VMEM((cols, width), jnp.bfloat16),
            pltpu.VMEM((n * rows, cols), jnp.float32),
            pltpu.SemaphoreType.DMA((len(spans), n + CORES * len(ints))),
            pltpu.SemaphoreType.DMA((n,)),
        ],
    )
    return pl.pallas_call(
        functools.partial(matmul_kernel, (n, len(ints)), rows, sub, spans, len(acc)),
        grid_spec=spec,
        out_shape=[jax.ShapeDtypeStruct((rows, cols), jnp.float32)] * n,
        compiler_params=pltpu.CompilerParams(vmem_limit_bytes=24 << 20),
        cost_estimate=pl.CostEstimate(
            flops=2 * n * rows * cols * width,
            bytes_accessed=2 * (n * rows + cols) * width,
            transcendentals=0,
        ),
        name="ladder_chunk",
    )(at, *amps, *ints, *acc)


def solution(mesh):
    n_pair, n_blk = mesh.shape["pair"], mesh.shape["blk"]
    chips = n_blk // CORES
    ring = ring_of(chips)
    long, short = chips // 2, chips - 1 - chips // 2

    def device(pair, chip, core):
        return pair * n_blk + chip * CORES + core

    def everywhere(target):
        return [
            (device(p, ch, c), device(*target(p, ch, c)))
            for p in range(n_pair)
            for ch in range(chips)
            for c in range(CORES)
        ]

    place = {ch: i for i, ch in enumerate(ring)}
    forward = everywhere(lambda p, ch, c: (p, ring[(place[ch] + 1) % chips], c))
    backward = everywhere(lambda p, ch, c: (p, ring[(place[ch] - 1) % chips], c))
    mates = [(d, e) for d in range(n_pair) for e in range(CORES)]
    to_mate = {
        (d, e): everywhere(lambda p, ch, c: ((p + d) % n_pair, ch, c ^ e)) for d, e in mates
    }
    grid = [(p, c) for p in range(n_pair) for c in range(CORES)]

    def send(x, pairs):
        return lax.ppermute(x, AXES, pairs)

    def choose(which, branch, *operands):
        return lax.switch(which, [functools.partial(branch, p, c) for p, c in grid], *operands)

    def per_device(amps, ints, block_of, pair_rows, occ_energy, vir_pair_energy):
        rows, total_width = amps.shape
        sub, width = ints.shape
        starts = [p * width // LANE * LANE for p in range(n_pair)]
        reach = max((p + 1) * width - starts[p] for p in range(n_pair))
        units = -(-reach // (LANE * CORES))
        half = units * LANE
        narrow, wide = chunks_of(units, n_pair)
        sizes = [u * LANE for u in narrow + ([wide] if wide else [])]
        offsets = [sum(sizes[:j]) for j in range(len(sizes))]
        count = len(narrow)
        pair, blk = lax.axis_index("pair"), lax.axis_index("blk")
        chip, core = blk // CORES, blk % CORES
        which = pair * CORES + core

        def amps_at(x, p, c, j):
            at = starts[p] + c * half + offsets[j]
            end = min(at + sizes[j], total_width)
            return jnp.pad(lax.slice(x, (0, at), (rows, end)), ((0, 0), (0, at + sizes[j] - end)))

        def amps_branch(j, some, p, c, x):
            return [amps_at(x, (p + d) % n_pair, c ^ e, j) for d, e in some]

        def wide_branch(p, c, x):
            return [
                jnp.concatenate(
                    [amps_at(x, (p + d) % n_pair, c ^ e, count) for d in range(n_pair)], axis=1
                )
                for e in range(CORES)
            ]

        def ints_branch(j, p, c, *slabs):
            shift = p * width - starts[p]
            first = c * half + offsets[j] - shift
            low, high = max(first, 0), min(first + sizes[j], width)
            column = p * width + low + lax.broadcasted_iota(jnp.int32, (1, high - low), 1)
            weight = jnp.where(column < NV, 1.0, 2.0).astype(jnp.bfloat16)
            both = jnp.concatenate([lax.slice(x, (0, low), (sub, high)) for x in slabs], axis=0)
            return jnp.pad(both * weight, ((0, 0), (low - first, first + sizes[j] - high)))

        def round_trip(piece, even):
            ahead, behind = (long, short) if even else (short, long)
            fwd, bwd = [piece], [piece]
            for s in range(1, max(ahead, behind) + 1):
                if s <= ahead:
                    fwd.append(send(fwd[-1], forward))
                if s <= behind:
                    bwd.append(send(bwd[-1], backward))
            return fwd + bwd[:0:-1]

        twin = send(ints, to_mate[(0, 1)])
        far = [m for m in mates if m[0] != 0]
        left, right = [], []
        for j in range(count):
            parts = choose(which, functools.partial(amps_branch, j, far), amps)
            parts = [pltpu.with_memory_space_constraint(x, pltpu.HBM) for x in parts]
            away = [send(x, to_mate[m]) for m, x in zip(far, parts)]
            near = mates[1:CORES]
            own = [amps]
            if sizes[j] < LARGE * LANE or starts[-1] + half + offsets[j] + sizes[j] > total_width:
                near, own = mates[:CORES], []
            parts = choose(which, functools.partial(amps_branch, j, near), amps)
            own += parts[:-1]
            left.append(own + [send(parts[-1], to_mate[(0, 1)])] + away)
            piece = choose(which, functools.partial(ints_branch, j), ints, twin)
            right.append(round_trip(piece, leads_forward(j)))
        if wide:
            piece = choose(which, functools.partial(ints_branch, count), ints, twin)
            others = [send(piece, to_mate[(n_pair - d, 0)]) for d in range(1, n_pair)]
            piece = jnp.concatenate([piece] + others, axis=1)
            right.append(round_trip(piece, leads_forward("w")))
            parts = choose(which, wide_branch, amps)
            left.append([parts[0], send(parts[1], to_mate[(0, 1)])])

        order = jnp.array(ring, jnp.int32)
        here = jnp.argmax(order == chip)
        behind_me = order[(here - jnp.arange(chips)) % chips]
        stored = jnp.stack([behind_me * CORES + core, behind_me * CORES + 1 - core], axis=1)
        pos = block_of[stored.reshape(-1)]
        first = jnp.array(starts, jnp.int32)[pair] + core * half
        at = [jnp.concatenate([first[None] + offset, pos]) for offset in offsets]

        acc = []
        for j in range(count):
            acc = chunk_matmul(at[j], left[j], right[j], acc, sizes[j])
        ladder = acc[0]
        for (d, e), part in list(zip(mates, acc))[1:]:
            ladder = ladder + send(part, to_mate[((n_pair - d) % n_pair, e)])
        if wide:
            acc = chunk_matmul(at[count], left[count], right[count], [], n_pair * sizes[count])
            ladder = ladder + acc[0] + send(acc[1], to_mate[(0, 1)])
        levels = lax.broadcasted_iota(jnp.int32, (1, 1, occ_energy.shape[0]), 2)
        one_hot = (pair_rows[:, :, None] == levels).astype(jnp.float32)
        occupied = jnp.sum(one_hot * occ_energy[None, None, :], axis=(1, 2))
        denominator = vir_pair_energy[None, :] - occupied[:, None]
        return ladder / denominator

    placed = (P(("blk", "pair"), None), P("blk", "pair"), P(), P(("blk", "pair"), None), P(), P())
    return jax.shard_map(per_device, mesh=mesh, in_specs=placed, out_specs=P(("blk", "pair"), None), check_vma=False)
```
